128 devices in a mesh: row: 8 (over x, core), col: 16 (over z, y).
Axes of the slice: x: 4, y: 4, z: 4, core: 2. Of those that a mesh axis runs over, the one named last changes fastest.
Arguments:
- hamiltonian: float32 [256, 4, 128, 128], P(('row', 'col')), may hold values from -20 to 20
- block_lists: int32 [256, 4], replicated, may hold values from -1 to 255, as said below
Outputs:
- density: float32 [256, 4, 128, 128], P(('row', 'col'))
The draws below stay inside these ranges and needn't reach their ends.
Inputs may be any that keep to these rules, and one draw needn't show every extreme that they name: `block_lists`: block column j = (r * 16 + c) * 2 + s sits on grid row r, grid column c, slot s. Entry 0 is j. Entry 1 is the column of the same r and s at grid column c - 1 (cyclically), entry 2 the one at c + 1, each either present or -1, present for both ends of a link or for neither. Entry 3 is never -1: the column of the same c and s on grid row r with one bit flipped, the same bit for all rows of one grid column and slot. Some columns have all four entries, some only entries 0 and 3.
All inputs are finite; a program needn't handle non-finite values.
Results may differ from the reference program's by a relative error of at most 0.0001.
Values sent between devices are 32-bit elements; how exact they have to be, the bound alone decides.
A program may use at most 64 MiB of HBM per device.

```python
import math
import jax
import jax.numpy as jnp
from jax import lax

B = 128
K = 4
COLS_DEV = 2
ITERS = 6
STEPS = 2
GRID_ROWS = 8
GRID_COLS = 16
NBLK = 256


def draw_block_lists(key, part):
    grid_rows = GRID_ROWS
    grid_cols = GRID_COLS
    slots_here = COLS_DEV
    edge_key, bit_key = jax.random.split(jax.random.fold_in(key, 7))
    link_on = jax.random.randint(edge_key, (grid_rows, grid_cols, slots_here), 0, 2)
    col_ids = jnp.arange(grid_cols, dtype=jnp.int32)[None, :, None]
    link_on = jnp.where(col_ids <= 1, 1, link_on)
    link_on = jnp.where((col_ids == 3) | (col_ids == 4), 0, link_on)
    bit_count = grid_rows.bit_length() - 1
    chosen = jax.random.randint(bit_key, (1, grid_cols, slots_here), 0, bit_count)
    row_ids = jnp.arange(grid_rows, dtype=jnp.int32)[:, None, None]
    slot_ids = jnp.arange(slots_here, dtype=jnp.int32)[None, None, :]

    def locate(row_pos, col_pos):
        return (row_pos * grid_cols + col_pos) * slots_here + slot_ids
    own_ids = locate(row_ids, col_ids)
    left_ids = jnp.where(jnp.roll(link_on, 1, axis=1) == 1, locate(row_ids, (col_ids - 1) % grid_cols), -1)
    right_ids = jnp.where(link_on == 1, locate(row_ids, (col_ids + 1) % grid_cols), -1)
    partner_ids = locate(jnp.bitwise_xor(row_ids, jnp.left_shift(jnp.int32(1), chosen)), col_ids)
    stacked = jnp.stack(jnp.broadcast_arrays(own_ids, left_ids, right_ids, partner_ids), -1)
    return stacked.reshape(NBLK, K).astype(jnp.int32)


def draw_hamiltonian(key, part):
    base_key = jax.random.fold_in(jax.random.fold_in(key, 11), 0)
    row_key = jax.random.fold_in(jax.random.fold_in(key, 11), 1)
    col_key = jax.random.fold_in(jax.random.fold_in(key, 11), 2)
    order_key = jax.random.fold_in(jax.random.fold_in(key, 11), 4)
    shape_all = (NBLK, K, B, B)
    devices = GRID_ROWS * GRID_COLS
    shuffled_rank = jax.random.permutation(order_key, devices)
    device_ids = jnp.arange(NBLK, dtype=jnp.int32) // COLS_DEV
    position = shuffled_rank[device_ids].astype(jnp.float32) / max(devices - 1, 1)
    ramp = 3.0 ** position
    values = jnp.clip(jax.random.normal(base_key, shape_all, jnp.float32), -5.0, 5.0)
    row_factor = jnp.exp(jax.random.uniform(row_key, (NBLK, K, B, 1), jnp.float32, -1.15, 1.15))
    col_factor = jnp.exp(jax.random.uniform(col_key, (NBLK, K, 1, B), jnp.float32, -1.15, 1.15))
    scaled = values * row_factor * col_factor * ramp[:, None, None, None] / math.sqrt(K * B)
    return jnp.clip(scaled, -19.5, 19.5).astype(jnp.float32)


def setup_inputs(seed: int = 0) -> dict:
    key_list = jax.random.split(jax.random.key(seed), 3)
    hamiltonian = draw_hamiltonian(jax.random.fold_in(key_list[2], 71), 0)
    block_lists = draw_block_lists(jax.random.fold_in(key_list[2], 71), 0)
    return dict(hamiltonian=hamiltonian, block_lists=block_lists)


facing = (0, 2, 1, 3)
epsilon = 1e-06

def symmetric(matrix):
    return 0.5 * (matrix + jnp.swapaxes(matrix, -1, -2))

def assemble(own_col, diagonals, face_blocks, present):
    column = 0.5 * (own_col + jnp.swapaxes(face_blocks, -1, -2)) * present[:, None, None]
    blocks = symmetric(diagonals) * present[:, None, None]
    side_len = own_col.shape[-1]
    members = own_col.shape[0]
    matrix = jnp.zeros((members, side_len, members, side_len), jnp.float32)
    matrix = matrix.at[0, :, 0, :].set(column[0])
    for position in range(1, members):
        matrix = matrix.at[position, :, 0, :].set(column[position])
        matrix = matrix.at[0, :, position, :].set(column[position].T)
        matrix = matrix.at[position, :, position, :].set(blocks[position])
    return matrix.reshape(members * side_len, members * side_len)

def sign_density(matrix, first_square, scaling, present):
    full_order = matrix.shape[0]
    identity = jnp.eye(full_order, dtype=jnp.float32)
    iterate = matrix * scaling
    square = first_square * (scaling * scaling)
    for repeat in range(ITERS):
        if repeat > 0:
            square = jnp.dot(iterate, iterate, precision=lax.Precision.HIGHEST)
        iterate = jnp.dot(iterate, 1.5 * identity - 0.5 * square, precision=lax.Precision.HIGHEST)
    central = 0.5 * (identity[:, :B] - iterate[:, :B])
    return central.reshape(K, B, B) * present[:, None, None]

def reference(hamiltonian, block_lists):
    present = (block_lists >= 0).astype(jnp.float32)
    columns = jnp.arange(NBLK, dtype=jnp.int32)
    safe_lists = jnp.where(block_lists >= 0, block_lists, columns[:, None]).astype(jnp.int32)
    face_index = jnp.array(facing, dtype=jnp.int32)
    member_ids = jnp.arange(K, dtype=jnp.int32)
    current = hamiltonian
    density = hamiltonian
    for scf_round in range(STEPS):

        def build_one(column):
            own_col = current[column]
            neighbours = current[safe_lists[column]]
            diagonals = neighbours[:, 0]
            face_blocks = neighbours[member_ids, face_index]
            return assemble(own_col, diagonals, face_blocks, present[column])

        def squares(column):
            matrix = build_one(column)
            square = jnp.dot(matrix, matrix, precision=lax.Precision.HIGHEST)
            return jnp.sum(square * square)
        largest = jnp.max(lax.map(squares, columns))
        scaling = 1.5 / jnp.sqrt(jnp.sqrt(largest + epsilon))

        def solve_one(column):
            matrix = build_one(column)
            square = jnp.dot(matrix, matrix, precision=lax.Precision.HIGHEST)
            return sign_density(matrix, square, scaling, present[column])
        density_cols = lax.map(solve_one, columns)
        density_face = density_cols[safe_lists, face_index[None, :]]
        density = 0.5 * (density_cols + jnp.swapaxes(density_face, -1, -2)) * present[:, :, None, None]
        current = hamiltonian + density
    return density
```

```python
import jax
import jax.numpy as jnp
from jax import lax
from jax.experimental import pallas as pl
from jax.experimental.pallas import tpu as pltpu
from jax.sharding import PartitionSpec as P

STEPS = 2
SLOTS = 2
B = 128
N = 512
T = 256
EPS = 1e-06
ROWS = 8
COLS = 16
f32 = jnp.float32
bf16 = jnp.bfloat16
MESH = pl.DeviceIdType.MESH


def dot(a, b):
    return jnp.dot(a, b, preferred_element_type=f32)


def put(ref, r, c, x):
    m, n = x.shape
    h = x.astype(bf16)
    ref[r : r + m, c : c + n] = h
    ref[r : r + m, N + c : N + c + n] = (x - h.astype(f32)).astype(bf16)


def put_symmetric(ref, f):
    put(ref, 0, 0, f[:T, :T])
    upper = f[:T, T:]
    put(ref, 0, T, upper)
    put(ref, T, 0, upper.T)
    put(ref, T, T, f[T:, T:])


def square(x, q, low):
    low[...] = dot(x[:, :N], x[:, N:])
    a = dot(x[:T, :N], x[:, :T])
    t00 = a + low[:T, :T] + low[:T, :T].T
    put(q, 0, 0, t00)
    a = dot(x[:, :N], x[:, T:N])
    t01 = a[:T] + low[:T, T:] + low[T:, :T].T
    put(q, 0, T, t01)
    put(q, T, 0, t01.T)
    t11 = a[T:] + low[T:, T:] + low[T:, T:].T
    put(q, T, T, t11)
    return t00, t01, t11


def product(x, q, store):
    for m, c in ((T, 0), (N, T)):
        h, l = x[:m, :N], x[:m, N:]
        qh, ql = q[:, c : c + T], q[:, N + c : N + c + T]
        store(m, c, dot(jnp.concatenate([h, h, l], 1), jnp.concatenate([qh, ql, qh], 0)))


def rowmul(v, q):
    h = v.astype(bf16)
    l = (v - h.astype(f32)).astype(bf16)
    p = dot(jnp.concatenate([h, l], 0), q[:, :N])
    return p[:B] + p[B:] + dot(h, q[:, N:])


def kernel(
    lists, h_any, out, hv, rb0, rb1, rb2, sm, fm, x0, q0, l0, x1, q1, l1, dct, dg, own1, own2, mx1, mx2,
    hsem, es, er, ms, mr,
):
    row, col = lax.axis_index("row"), lax.axis_index("col")
    rb = (rb0, rb1, rb2)
    xs, qs, ls = (x0, x1), (q0, q1), (l0, l1)
    row_c = row + 1 - 2 * (row % 2)
    row_x = row + 2 - 4 * ((row // 2) % 2)
    row_f = (row_x + 4) % ROWS

    load = pltpu.make_async_copy(h_any, hv, hsem)
    load.start()
    barrier = pltpu.get_barrier_semaphore()
    for d in range(1, ROWS):
        pl.semaphore_signal(barrier, inc=1, device_id=((row + d) % ROWS, col), device_id_type=MESH)
    for d in range(1, COLS):
        pl.semaphore_signal(barrier, inc=1, device_id=(row, (col + d) % COLS), device_id_type=MESH)

    def cp(e, d, s, q):
        target = (
            (row, (col + 1) % COLS),
            (row, (col + COLS - 1) % COLS),
            (row_c, col),
            (row_x, col),
            (row_f, col),
        )[d]
        face = (2, 1, 3, 3, 3)[d]
        if d == 4:
            src = rb[e].at[3, s, q]
        elif e == 0:
            src = hv.at[s, face if q else 0]
        elif e == 1:
            src = dct.at[0, s, face] if q else dg.at[0, s]
        else:
            src = dct.at[1, s, face, pl.ds(64 * q, 64)]
        return pltpu.make_async_remote_copy(
            src_ref=src,
            dst_ref=rb[e].at[d, s, q],
            send_sem=es.at[e, d, s, q],
            recv_sem=er.at[e, d, s, q],
            device_id=target,
            device_id_type=MESH,
        )

    def send(e, s):
        for q in range(2):
            for d in (3, 0, 1, 2):
                cp(e, d, s, q).start()

    def relay(e, s):
        for q in range(2):
            cp(e, 3, s, q).wait_recv()
            cp(e, 4, s, q).start()

    def arrived(e, s, dirs):
        for d in dirs:
            for q in range(2):
                cp(e, d, s, q).wait_recv()

    def maxcp(t, k):
        if k < ROWS:
            src, dst, target = own1.at[t], mx1.at[t, k], ((row + k) % ROWS, col)
        else:
            d = k - ROWS + 1
            src, dst, target = own2.at[t], mx2.at[t, d], (row, (col + d) % COLS)
        return pltpu.make_async_remote_copy(
            src_ref=src, dst_ref=dst, send_sem=ms.at[t, k], recv_sem=mr.at[t, k], device_id=target, device_id_type=MESH
        )

    present, chosen = [], []
    for s in range(SLOTS):
        j = (row * COLS + col) * SLOTS + s
        present.append([1.0] + [jnp.where(lists[j, k] >= 0, 1.0, 0.0).astype(f32) for k in range(1, 4)])
        apart = jnp.abs(lists[j, 3] // (SLOTS * COLS) - row)
        chosen.append((apart < 2, apart < 4))

    def got(e, s, k, q):
        if k < 3:
            return rb[e][k - 1, s, q]
        near, mid = chosen[s]
        return jnp.where(near, rb[e][2, s, q], jnp.where(mid, rb[e][3, s, q], rb[e][4, s, q]))

    blk = [slice(B * k, B * k + B) for k in range(4)]

    def assemble(t, s):
        x = xs[s]
        if t == 0:
            h = hv[s, 0]
            d = 0.5 * (h + h.T)
        else:
            d = sm[s, blk[0], blk[0]] + dg[0, s]
        sm[s, blk[0], blk[0]] = d
        put(x, 0, 0, d)
        for k in range(1, 4):
            p = present[s][k]
            diag, face = got(t, s, k, 0), got(t, s, k, 1)
            if t == 0:
                low = (0.5 * p) * (hv[s, k] + face.T)
                d = (0.5 * p) * (diag + diag.T)
            else:
                low = sm[s, blk[k], blk[0]] + (0.5 * p) * (dct[0, s, k].T + face)
                d = sm[s, blk[k], blk[k]] + p * diag
            up = low.T
            sm[s, blk[k], blk[0]] = low
            sm[s, blk[0], blk[k]] = up
            sm[s, blk[k], blk[k]] = d
            put(x, B * k, 0, low)
            put(x, 0, B * k, up)
            put(x, B * k, B * k, d)
            for i in range(1, 4):
                if t != 0 and i != k:
                    put(x, B * k, B * i, jnp.zeros((B, B), f32))

    def combine(s, alpha, beta):
        for r, c in ((0, 0), (0, T), (T, T)):
            f = alpha * sm[s, r : r + T, c : c + T] - beta * fm[s, r : r + T, c : c + T]
            fm[s, r : r + T, c : c + T] = f
            put(xs[s], r, c, f)
            if r != c:
                put(xs[s], c, r, f.T)

    def cube(s):
        def store(m, c, p):
            fm[s, :m, c : c + T] = p

        product(xs[s], qs[s], store)

    def advance(s):
        def store(m, c, p):
            fm[s, :m, c : c + T] = 1.5 * fm[s, :m, c : c + T] - 0.5 * p

        product(xs[s], qs[s], store)
        put_symmetric(xs[s], fm[s])

    def sq(s):
        return square(xs[s], qs[s], ls[s])

    def norm(s):
        t00, t01, t11 = sq(s)
        total = t00 * t00 + 2.0 * (t01 * t01) + t11 * t11
        return jnp.sum(total, axis=(0, 1), keepdims=True)

    def tail(t, s):
        y = qs[s]
        v = fm[s, :B, :]
        w = 1.5 * v - 0.5 * rowmul(v, y)
        a = rowmul(w, y)
        a = 1.5 * a - 0.5 * rowmul(a, y)
        a = 1.5 * a - 0.5 * rowmul(a, y)
        z = 1.5 * w - 0.5 * a
        eye = (lax.broadcasted_iota(jnp.int32, (B, B), 0) == lax.broadcasted_iota(jnp.int32, (B, B), 1)).astype(f32)
        centre = 0.5 * (eye - z[:, blk[0]])
        dg[t, s] = 0.5 * (centre + centre.T)
        for k in range(1, 4):
            dct[t, s, k] = (-0.5 * present[s][k]) * z[:, blk[k]]

    for x in xs:
        x[...] = jnp.zeros_like(x)
    sm[...] = jnp.zeros_like(sm)
    load.wait()
    pl.semaphore_wait(barrier, ROWS + COLS - 2)

    for s in range(SLOTS):
        send(0, s)
    for s in range(SLOTS):
        relay(0, s)

    for t in range(STEPS):
        arrived(t, 0, (0, 1, 2, 4))
        assemble(t, 0)
        n0 = norm(0)
        if t == 1:
            relay(1, 1)
        arrived(t, 1, (0, 1, 2, 4))
        assemble(t, 1)
        n1 = norm(1)
        own1[t] = jnp.broadcast_to(jnp.maximum(n0, n1), (8, 128))
        for k in range(1, ROWS):
            maxcp(t, k).start()
        cube(0)
        for k in range(1, ROWS):
            maxcp(t, k).wait_recv()
        top = own1[t]
        for k in range(1, ROWS):
            top = jnp.maximum(top, mx1[t, k])
        own2[t] = top
        for k in range(ROWS, ROWS + COLS - 1):
            maxcp(t, k).start()
        cube(1)
        for k in range(ROWS, ROWS + COLS - 1):
            maxcp(t, k).wait_recv()
            top = jnp.maximum(top, mx2[t, k - ROWS + 1])
        scale = 1.5 / jnp.sqrt(jnp.sqrt(top + EPS))
        alpha = (1.5 * scale)[:1, :1]
        beta = (0.5 * scale * scale * scale)[:1, :1]
        combine(0, alpha, beta)
        combine(1, alpha, beta)
        sq(0)

        def body(i, carry):
            advance(0)
            sq(1)
            sq(0)
            advance(1)
            return carry

        lax.fori_loop(0, 3, body, 0)
        tail(t, 0)
        send(t + 1, 0)
        sq(1)
        tail(t, 1)
        send(t + 1, 1)
        relay(t + 1, 0)

    def finish(s):
        arrived(2, s, (0, 1, 2, 4))
        out[s, 0] = dg[1, s]
        for k in range(1, 4):
            face = jnp.concatenate([got(2, s, k, 0), got(2, s, k, 1)], 0)
            out[s, k] = (0.5 * present[s][k]) * (dct[1, s, k].T + face)

    relay(2, 1)
    for s in range(SLOTS):
        finish(s)

    for e in range(STEPS + 1):
        for s in range(SLOTS):
            for d in range(5):
                for q in range(2):
                    cp(e, d, s, q).wait_send()
    for t in range(STEPS):
        for k in range(1, ROWS + COLS - 1):
            maxcp(t, k).wait_send()


def per_device(hamiltonian, block_lists):
    mat = pltpu.VMEM((N, N), f32)
    halves = pltpu.VMEM((N, 2 * N), bf16)
    return pl.pallas_call(
        kernel,
        out_shape=jax.ShapeDtypeStruct((SLOTS, 4, B, B), f32),
        in_specs=[pl.BlockSpec(memory_space=pltpu.SMEM), pl.BlockSpec(memory_space=pl.ANY)],
        out_specs=pl.BlockSpec(memory_space=pltpu.VMEM),
        scratch_shapes=[
            pltpu.VMEM((SLOTS, 4, B, B), f32),
            pltpu.VMEM((5, SLOTS, 2, B, B), f32),
            pltpu.VMEM((5, SLOTS, 2, B, B), f32),
            pltpu.VMEM((5, SLOTS, 2, B // 2, B), f32),
            pltpu.VMEM((SLOTS, N, N), f32),
            pltpu.VMEM((SLOTS, N, N), f32),
            halves, halves, mat,
            halves, halves, mat,
            pltpu.VMEM((STEPS, SLOTS, 4, B, B), f32),
            pltpu.VMEM((STEPS, SLOTS, B, B), f32),
            pltpu.VMEM((STEPS, 8, 128), f32),
            pltpu.VMEM((STEPS, 8, 128), f32),
            pltpu.VMEM((STEPS, ROWS, 8, 128), f32),
            pltpu.VMEM((STEPS, COLS, 8, 128), f32),
            pltpu.SemaphoreType.DMA,
            pltpu.SemaphoreType.DMA((3, 5, SLOTS, 2)),
            pltpu.SemaphoreType.DMA((3, 5, SLOTS, 2)),
            pltpu.SemaphoreType.DMA((STEPS, ROWS + COLS - 1)),
            pltpu.SemaphoreType.DMA((STEPS, ROWS + COLS - 1)),
        ],
        compiler_params=pltpu.CompilerParams(collective_id=0, has_side_effects=True),
    )(block_lists, hamiltonian)


def solution(mesh):
    return jax.shard_map(
        per_device,
        mesh=mesh,
        in_specs=(P(("row", "col"), None, None, None), P()),
        out_specs=P(("row", "col"), None, None, None),
        check_vma=False,
    )
```

```python
import jax
import jax.numpy as jnp
from jax import lax
from jax.experimental import pallas as pl
from jax.experimental.pallas import tpu as pltpu
from jax.sharding import PartitionSpec as P

STEPS = 2
SLOTS = 2
B = 128
N = 512
T = 256
EPS = 1e-06
ROWS = 8
COLS = 16
f32 = jnp.float32
bf16 = jnp.bfloat16
MESH = pl.DeviceIdType.MESH


def dot(a, b):
    return jnp.dot(a, b, preferred_element_type=f32)


def put(ref, r, c, x):
    m, n = x.shape
    h = x.astype(bf16)
    ref[r : r + m, c : c + n] = h
    ref[r : r + m, N + c : N + c + n] = (x - h.astype(f32)).astype(bf16)


def put_symmetric(ref, f):
    put(ref, 0, 0, f[:T, :T])
    upper = f[:T, T:]
    put(ref, 0, T, upper)
    put(ref, T, 0, upper.T)
    put(ref, T, T, f[T:, T:])


def square(x, q, low):
    low[...] = dot(x[:, :N], x[:, N:])
    a = dot(x[:T, :N], x[:, :T])
    t00 = a + low[:T, :T] + low[:T, :T].T
    put(q, 0, 0, t00)
    a = dot(x[:, :N], x[:, T:N])
    t01 = a[:T] + low[:T, T:] + low[T:, :T].T
    put(q, 0, T, t01)
    put(q, T, 0, t01.T)
    t11 = a[T:] + low[T:, T:] + low[T:, T:].T
    put(q, T, T, t11)
    return t00, t01, t11


def product(x, q, store):
    for m, c in ((T, 0), (N, T)):
        h, l = x[:m, :N], x[:m, N:]
        qh, ql = q[:, c : c + T], q[:, N + c : N + c + T]
        store(m, c, dot(jnp.concatenate([h, h, l], 1), jnp.concatenate([qh, ql, qh], 0)))


def rowmul(v, q):
    h = v.astype(bf16)
    l = (v - h.astype(f32)).astype(bf16)
    p = dot(jnp.concatenate([h, l], 0), q[:, :N])
    return p[:B] + p[B:] + dot(h, q[:, N:])


def kernel(
    lists, h_any, out, hv, rb0, rb1, rb2, sm, fm, pw, x0, q0, l0, c0, d0, e0, x1, q1, l1, c1, d1, e1, dct, dg, own1, own2, mx1, mx2,
    hsem, es, er, ms, mr,
):
    row, col = lax.axis_index("row"), lax.axis_index("col")
    rb = (rb0, rb1, rb2)
    xs, qs, ls = (x0, x1), (q0, q1), (l0, l1)
    thirds, fourths, fifths = (c0, c1), (d0, d1), (e0, e1)
    row_c = row + 1 - 2 * (row % 2)
    row_x = row + 2 - 4 * ((row // 2) % 2)
    row_f = (row_x + 4) % ROWS

    def row_peer(k):
        return (2 * ((row // 2 + k // 2) % 4) + (row % 2 + k % 2) % 2, col)

    def col_peer(k):
        return (row, 4 * ((col // 4 + k // 4) % 4) + (col % 4 + k % 4) % 4)

    def hops(n):
        return min(n, 4 - n)

    row_order = sorted(range(1, ROWS), key=lambda k: -hops(k // 2) - k % 2 / 4)
    col_order = [ROWS + k for k in sorted(range(1, COLS), key=lambda k: -hops(k // 4) - hops(k % 4))]

    load = pltpu.make_async_copy(h_any, hv, hsem)
    load.start()
    barrier = pltpu.get_barrier_semaphore()
    for k in col_order:
        pl.semaphore_signal(barrier, inc=1, device_id=col_peer(k - ROWS), device_id_type=MESH)
    for k in row_order:
        pl.semaphore_signal(barrier, inc=1, device_id=row_peer(k), device_id_type=MESH)

    def cp(e, d, s, q):
        target = (
            (row, (col + 1) % COLS),
            (row, (col + COLS - 1) % COLS),
            (row_c, col),
            (row_x, col),
            (row_f, col),
        )[d]
        face = (2, 1, 3, 3, 3)[d]
        if d == 4:
            src = rb[e].at[3, s, q]
        elif e == 0:
            src = hv.at[s, face if q else 0]
        elif e == 1:
            src = dct.at[0, s, face] if q else dg.at[0, s]
        else:
            src = dct.at[1, s, face, pl.ds(64 * q, 64)]
        return pltpu.make_async_remote_copy(
            src_ref=src,
            dst_ref=rb[e].at[d, s, q],
            send_sem=es.at[e, d, s, q],
            recv_sem=er.at[e, d, s, q],
            device_id=target,
            device_id_type=MESH,
        )

    def send(e, s):
        for q in range(2):
            for d in (3, 0, 1, 2):
                cp(e, d, s, q).start()

    def relay(e, s):
        for q in range(2):
            cp(e, 3, s, q).wait_recv()
            cp(e, 4, s, q).start()

    def arrived(e, s, dirs):
        for d in dirs:
            for q in range(2):
                cp(e, d, s, q).wait_recv()

    def sent(e):
        for s in range(SLOTS):
            for d in range(5):
                for q in range(2):
                    cp(e, d, s, q).wait_send()

    def maxcp(t, k):
        if k < ROWS:
            src, dst, target = own1.at[t], mx1.at[t, k], row_peer(k)
        else:
            src, dst, target = own2.at[t], mx2.at[t, k - ROWS], col_peer(k - ROWS)
        return pltpu.make_async_remote_copy(
            src_ref=src, dst_ref=dst, send_sem=ms.at[t, k], recv_sem=mr.at[t, k], device_id=target, device_id_type=MESH
        )

    present, chosen = [], []
    for s in range(SLOTS):
        j = (row * COLS + col) * SLOTS + s
        present.append([1.0] + [jnp.where(lists[k, j] >= 0, 1.0, 0.0).astype(f32) for k in range(1, 4)])
        apart = jnp.abs(lists[3, j] // (SLOTS * COLS) - row)
        chosen.append((apart < 2, apart < 4))

    def got(e, s, k, q):
        if k < 3:
            return rb[e][k - 1, s, q]
        near, mid = chosen[s]
        return jnp.where(near, rb[e][2, s, q], jnp.where(mid, rb[e][3, s, q], rb[e][4, s, q]))

    blk = [slice(B * k, B * k + B) for k in range(4)]

    def assemble(t, s):
        x = xs[s]
        if t == 0:
            h = hv[s, 0]
            d = 0.5 * (h + h.T)
        else:
            d = sm[s, blk[0], blk[0]] + dg[0, s]
        sm[s, blk[0], blk[0]] = d
        put(x, 0, 0, d)
        for k in range(1, 4):
            p = present[s][k]
            diag, face = got(t, s, k, 0), got(t, s, k, 1)
            if t == 0:
                low = (0.5 * p) * (hv[s, k] + face.T)
                d = (0.5 * p) * (diag + diag.T)
            else:
                low = sm[s, blk[k], blk[0]] + (0.5 * p) * (dct[0, s, k].T + face)
                d = sm[s, blk[k], blk[k]] + p * diag
            up = low.T
            sm[s, blk[k], blk[0]] = low
            sm[s, blk[0], blk[k]] = up
            sm[s, blk[k], blk[k]] = d
            put(x, B * k, 0, low)
            put(x, 0, B * k, up)
            put(x, B * k, B * k, d)
            for i in range(1, 4):
                if t != 0 and i != k:
                    put(x, B * k, B * i, jnp.zeros((B, B), f32))

    def combine(s, scale):
        two = scale * scale
        c1 = 2.25 * scale
        c3 = -2.4375 * scale * two
        c5 = 1.6875 * scale * (two * two)
        c7 = -0.5625 * scale * (two * two) * two
        c9 = 0.0625 * scale * (two * two) * (two * two)
        for r, c in ((0, 0), (0, T), (T, T)):
            at = (s, slice(r, r + T), slice(c, c + T))
            f = c1 * sm[at] + c3 * fm[at] + c5 * pw[(0, *at)] + c7 * pw[(1, *at)] + c9 * pw[(2, *at)]
            fm[at] = f
            put(xs[s], r, c, f)
            if r != c:
                put(xs[s], c, r, f.T)

    def power(a, b, s, dst, halves=None):
        def store(m, c, p):
            dst[s, :m, c : c + T] = p
            if halves is not None:
                put(halves, 0, c, p)
                if c:
                    put(halves, T, 0, p[:T].T)

        product(a, b, store)

    def cube(s):
        power(xs[s], qs[s], s, fm, thirds[s])

    def fourth(s):
        square(qs[s], fourths[s], ls[s])

    def fifth(s):
        power(thirds[s], qs[s], s, pw.at[0], fifths[s])

    def seventh(s):
        power(thirds[s], fourths[s], s, pw.at[1])

    def ninth(s):
        power(fifths[s], fourths[s], s, pw.at[2])

    def advance(s):
        def store(m, c, p):
            fm[s, :m, c : c + T] = 1.5 * fm[s, :m, c : c + T] - 0.5 * p

        product(xs[s], qs[s], store)
        put_symmetric(xs[s], fm[s])

    def sq(s):
        return square(xs[s], qs[s], ls[s])

    def norm(s):
        t00, t01, t11 = sq(s)
        total = t00 * t00 + 2.0 * (t01 * t01) + t11 * t11
        return jnp.sum(total, axis=(0, 1), keepdims=True)

    def tail(t, s):
        y = qs[s]
        v = fm[s, :B, :]
        w = 1.5 * v - 0.5 * rowmul(v, y)
        a = rowmul(w, y)
        a = 1.5 * a - 0.5 * rowmul(a, y)
        a = 1.5 * a - 0.5 * rowmul(a, y)
        z = 1.5 * w - 0.5 * a
        eye = (lax.broadcasted_iota(jnp.int32, (B, B), 0) == lax.broadcasted_iota(jnp.int32, (B, B), 1)).astype(f32)
        centre = 0.5 * (eye - z[:, blk[0]])
        dg[t, s] = 0.5 * (centre + centre.T)
        for k in range(1, 4):
            dct[t, s, k] = (-0.5 * present[s][k]) * z[:, blk[k]]

    for x in xs:
        x[...] = jnp.zeros_like(x)
    sm[...] = jnp.zeros_like(sm)
    load.wait()
    pl.semaphore_wait(barrier, ROWS + COLS - 2)

    for s in range(SLOTS):
        send(0, s)
    for s in range(SLOTS):
        relay(0, s)

    for t in range(STEPS):
        arrived(t, 0, (0, 1, 2, 4))
        assemble(t, 0)
        n0 = norm(0)
        if t == 1:
            relay(1, 1)
        cube(0)
        fourth(0)
        arrived(t, 1, (0, 1, 2, 4))
        assemble(t, 1)
        n1 = norm(1)
        own1[t] = jnp.broadcast_to(jnp.maximum(n0, n1), (8, 128))
        for k in row_order:
            maxcp(t, k).start()
        cube(1)
        fifth(0)
        fourth(1)
        seventh(0)
        for k in row_order:
            maxcp(t, k).wait_recv()
        top = own1[t]
        for k in row_order:
            top = jnp.maximum(top, mx1[t, k])
        own2[t] = top
        for k in col_order:
            maxcp(t, k).start()
        fifth(1)
        ninth(0)
        seventh(1)
        ninth(1)
        sent(t)
        for k in row_order:
            maxcp(t, k).wait_send()
        for k in col_order:
            maxcp(t, k).wait_recv()
            top = jnp.maximum(top, mx2[t, k - ROWS])
        scale = (1.5 / jnp.sqrt(jnp.sqrt(top + EPS)))[:1, :1]
        combine(0, scale)
        combine(1, scale)
        sq(0)

        def body(i, carry):
            advance(0)
            sq(1)
            sq(0)
            advance(1)
            return carry

        lax.fori_loop(0, 2, body, 0)
        tail(t, 0)
        send(t + 1, 0)
        sq(1)
        tail(t, 1)
        send(t + 1, 1)
        relay(t + 1, 0)

    def finish(s):
        arrived(2, s, (0, 1, 2, 4))
        out[s, 0] = dg[1, s]
        for k in range(1, 4):
            face = jnp.concatenate([got(2, s, k, 0), got(2, s, k, 1)], 0)
            out[s, k] = (0.5 * present[s][k]) * (dct[1, s, k].T + face)

    relay(2, 1)
    for s in range(SLOTS):
        finish(s)

    for t in range(STEPS):
        for k in col_order:
            maxcp(t, k).wait_send()
    sent(STEPS)


def per_device(hamiltonian, block_lists):
    mat = pltpu.VMEM((N, N), f32)
    halves = pltpu.VMEM((N, 2 * N), bf16)
    return pl.pallas_call(
        kernel,
        out_shape=jax.ShapeDtypeStruct((SLOTS, 4, B, B), f32),
        in_specs=[pl.BlockSpec(memory_space=pltpu.SMEM), pl.BlockSpec(memory_space=pl.ANY)],
        out_specs=pl.BlockSpec(memory_space=pltpu.VMEM),
        scratch_shapes=[
            pltpu.VMEM((SLOTS, 4, B, B), f32),
            pltpu.VMEM((5, SLOTS, 2, B, B), f32),
            pltpu.VMEM((5, SLOTS, 2, B, B), f32),
            pltpu.VMEM((5, SLOTS, 2, B // 2, B), f32),
            pltpu.VMEM((SLOTS, N, N), f32),
            pltpu.VMEM((SLOTS, N, N), f32),
            pltpu.VMEM((3, SLOTS, N, N), f32),
            halves, halves, mat, halves, halves, halves,
            halves, halves, mat, halves, halves, halves,
            pltpu.VMEM((STEPS, SLOTS, 4, B, B), f32),
            pltpu.VMEM((STEPS, SLOTS, B, B), f32),
            pltpu.VMEM((STEPS, 8, 128), f32),
            pltpu.VMEM((STEPS, 8, 128), f32),
            pltpu.VMEM((STEPS, ROWS, 8, 128), f32),
            pltpu.VMEM((STEPS, COLS, 8, 128), f32),
            pltpu.SemaphoreType.DMA,
            pltpu.SemaphoreType.DMA((3, 5, SLOTS, 2)),
            pltpu.SemaphoreType.DMA((3, 5, SLOTS, 2)),
            pltpu.SemaphoreType.DMA((STEPS, ROWS + COLS)),
            pltpu.SemaphoreType.DMA((STEPS, ROWS + COLS)),
        ],
        compiler_params=pltpu.CompilerParams(collective_id=0, has_side_effects=True),
    )(block_lists.T, hamiltonian)


def solution(mesh):
    return jax.shard_map(
        per_device,
        mesh=mesh,
        in_specs=(P(("row", "col"), None, None, None), P()),
        out_specs=P(("row", "col"), None, None, None),
        check_vma=False,
    )
```

```python
import jax
import jax.numpy as jnp
from jax import lax
from jax.experimental import pallas as pl
from jax.experimental.pallas import tpu as pltpu
from jax.sharding import PartitionSpec as P

STEPS = 2
SLOTS = 2
B = 128
N = 512
T = 256
EPS = 1e-06
ROWS = 8
COLS = 16
f32 = jnp.float32
bf16 = jnp.bfloat16
MESH = pl.DeviceIdType.MESH


def dot(a, b):
    return jnp.dot(a, b, preferred_element_type=f32)


def put(ref, r, c, x):
    m, n = x.shape
    h = x.astype(bf16)
    ref[r : r + m, c : c + n] = h
    ref[r : r + m, N + c : N + c + n] = (x - h.astype(f32)).astype(bf16)


def put_symmetric(ref, f):
    put(ref, 0, 0, f[:T, :T])
    upper = f[:T, T:]
    put(ref, 0, T, upper)
    put(ref, T, 0, upper.T)
    put(ref, T, T, f[T:, T:])


def square(x, q, low):
    low[...] = dot(x[:, :N], x[:, N:])
    a = dot(x[:T, :N], x[:, :T])
    t00 = a + low[:T, :T] + low[:T, :T].T
    put(q, 0, 0, t00)
    a = dot(x[:, :N], x[:, T:N])
    t01 = a[:T] + low[:T, T:] + low[T:, :T].T
    put(q, 0, T, t01)
    put(q, T, 0, t01.T)
    t11 = a[T:] + low[T:, T:] + low[T:, T:].T
    put(q, T, T, t11)
    return t00, t01, t11


def product(x, q, store):
    for m, c in ((T, 0), (N, T)):
        h, l = x[:m, :N], x[:m, N:]
        qh, ql = q[:, c : c + T], q[:, N + c : N + c + T]
        store(m, c, dot(jnp.concatenate([h, h, l], 1), jnp.concatenate([qh, ql, qh], 0)))


def rowmul(v, q):
    h = v.astype(bf16)
    l = (v - h.astype(f32)).astype(bf16)
    p = dot(jnp.concatenate([h, l], 0), q[:, :N])
    return p[:B] + p[B:] + dot(h, q[:, N:])


def kernel(
    lists, h_any, out, hv, rb0, rb1, rb2, sm, fm, pw, x0, q0, l0, c0, d0, e0, x1, q1, l1, c1, d1, e1, dct, dg, own1, own2, mx1, mx2,
    hsem, es, er, ms, mr,
):
    row, col = lax.axis_index("row"), lax.axis_index("col")
    rb = (rb0, rb1, rb2)
    xs, qs, ls = (x0, x1), (q0, q1), (l0, l1)
    thirds, fourths, fifths = (c0, c1), (d0, d1), (e0, e1)
    row_c = row + 1 - 2 * (row % 2)
    row_x = row + 2 - 4 * ((row // 2) % 2)
    row_f = (row_x + 4) % ROWS

    def row_peer(k):
        return (2 * ((row // 2 + k // 2) % 4) + (row % 2 + k % 2) % 2, col)

    def col_peer(k):
        return (row, 4 * ((col // 4 + k // 4) % 4) + (col % 4 + k % 4) % 4)

    def hops(n):
        return min(n, 4 - n)

    row_order = sorted(range(1, ROWS), key=lambda k: -hops(k // 2) - k % 2 / 4)
    col_order = [ROWS + k for k in sorted(range(1, COLS), key=lambda k: -hops(k // 4) - hops(k % 4))]

    load = pltpu.make_async_copy(h_any, hv, hsem)
    load.start()
    barrier = pltpu.get_barrier_semaphore()
    for k in col_order:
        pl.semaphore_signal(barrier, inc=1, device_id=col_peer(k - ROWS), device_id_type=MESH)
    for k in row_order:
        pl.semaphore_signal(barrier, inc=1, device_id=row_peer(k), device_id_type=MESH)

    def pieces(e, d):
        return 4 if d >= 3 and e < STEPS else 2

    def cp(e, d, s, c):
        target = (
            (row, (col + 1) % COLS),
            (row, (col + COLS - 1) % COLS),
            (row_c, col),
            (row_x, col),
            (row_f, col),
        )[d]
        face = (2, 1, 3, 3, 3)[d]
        half = B // 2
        fine = pieces(e, d) == 4
        q = c // 2 if fine else c
        part = pl.ds(half * (c % 2), half)
        if d == 4:
            src = rb[e].at[3, s, q]
        elif e == 0:
            src = hv.at[s, face if q else 0]
        elif e == 1:
            src = dct.at[0, s, face] if q else dg.at[0, s]
        else:
            src = dct.at[1, s, face, pl.ds(half * q, half)]
        dst = rb[e].at[d, s, q]
        return pltpu.make_async_remote_copy(
            src_ref=src.at[part] if fine else src,
            dst_ref=dst.at[part] if fine else dst,
            send_sem=es.at[e, d, s, c],
            recv_sem=er.at[e, d, s, c],
            device_id=target,
            device_id_type=MESH,
        )

    def send(e, s):
        for c in range(4):
            for d in (3, 0, 1, 2):
                if c < pieces(e, d):
                    cp(e, d, s, c).start()

    def relay(e, s):
        for c in range(pieces(e, 3)):
            cp(e, 3, s, c).wait_recv()
            cp(e, 4, s, c).start()

    def arrived(e, s, dirs):
        for d in dirs:
            for c in range(pieces(e, d)):
                cp(e, d, s, c).wait_recv()

    def sent(e):
        for s in range(SLOTS):
            for d in range(5):
                for c in range(pieces(e, d)):
                    cp(e, d, s, c).wait_send()

    def maxcp(t, k):
        if k < ROWS:
            src, dst, target = own1.at[t], mx1.at[t, k], row_peer(k)
        else:
            src, dst, target = own2.at[t], mx2.at[t, k - ROWS], col_peer(k - ROWS)
        return pltpu.make_async_remote_copy(
            src_ref=src, dst_ref=dst, send_sem=ms.at[t, k], recv_sem=mr.at[t, k], device_id=target, device_id_type=MESH
        )

    present, chosen = [], []
    for s in range(SLOTS):
        j = (row * COLS + col) * SLOTS + s
        present.append([1.0] + [jnp.where(lists[k, j] >= 0, 1.0, 0.0).astype(f32) for k in range(1, 4)])
        apart = jnp.abs(lists[3, j] // (SLOTS * COLS) - row)
        chosen.append((apart < 2, apart < 4))

    def got(e, s, k, q):
        if k < 3:
            return rb[e][k - 1, s, q]
        near, mid = chosen[s]
        return jnp.where(near, rb[e][2, s, q], jnp.where(mid, rb[e][3, s, q], rb[e][4, s, q]))

    blk = [slice(B * k, B * k + B) for k in range(4)]

    def assemble(t, s):
        x = xs[s]
        if t == 0:
            h = hv[s, 0]
            d = 0.5 * (h + h.T)
            sm[s, blk[0], blk[0]] = d
        else:
            d = sm[s, blk[0], blk[0]]
        put(x, 0, 0, d)
        for k in range(1, 4):
            p = present[s][k]
            diag, face = got(t, s, k, 0), got(t, s, k, 1)
            if t == 0:
                low = (0.5 * p) * (hv[s, k] + face.T)
                d = (0.5 * p) * (diag + diag.T)
            else:
                low = sm[s, blk[k], blk[0]] + (0.5 * p) * face
                d = sm[s, blk[k], blk[k]] + p * diag
            up = low.T
            sm[s, blk[k], blk[0]] = low
            sm[s, blk[0], blk[k]] = up
            sm[s, blk[k], blk[k]] = d
            put(x, B * k, 0, low)
            put(x, 0, B * k, up)
            put(x, B * k, B * k, d)

    def prepare(t, s):
        if t == 0:
            sm[s, blk[0], blk[0]] = sm[s, blk[0], blk[0]] + dg[0, s]
        else:
            out[s, 0] = dg[1, s]
        for k in range(1, 4):
            own = (0.5 * present[s][k]) * dct[t, s, k].T
            if t == 0:
                sm[s, blk[k], blk[0]] = sm[s, blk[k], blk[0]] + own
                for i in range(1, 4):
                    if i != k:
                        put(xs[s], B * k, B * i, jnp.zeros((B, B), f32))
            else:
                out[s, k] = own

    def combine(s, scale):
        two = scale * scale
        c1 = 2.25 * scale
        c3 = -2.4375 * scale * two
        c5 = 1.6875 * scale * (two * two)
        c7 = -0.5625 * scale * (two * two) * two
        c9 = 0.0625 * scale * (two * two) * (two * two)
        for r, c in ((0, 0), (0, T), (T, T)):
            at = (s, slice(r, r + T), slice(c, c + T))
            f = c1 * sm[at] + c3 * fm[at] + c5 * pw[(0, *at)] + c7 * pw[(1, *at)] + c9 * pw[(2, *at)]
            fm[at] = f
            put(xs[s], r, c, f)
            if r != c:
                put(xs[s], c, r, f.T)

    def power(a, b, s, dst, halves=None):
        def store(m, c, p):
            dst[s, :m, c : c + T] = p
            if halves is not None:
                put(halves, 0, c, p)
                if c:
                    put(halves, T, 0, p[:T].T)

        product(a, b, store)

    def cube(s):
        power(xs[s], qs[s], s, fm, thirds[s])

    def fourth(s):
        square(qs[s], fourths[s], ls[s])

    def fifth(s):
        power(thirds[s], qs[s], s, pw.at[0], fifths[s])

    def seventh(s):
        power(thirds[s], fourths[s], s, pw.at[1])

    def ninth(s):
        power(fifths[s], fourths[s], s, pw.at[2])

    def advance(s):
        def store(m, c, p):
            fm[s, :m, c : c + T] = 1.5 * fm[s, :m, c : c + T] - 0.5 * p

        product(xs[s], qs[s], store)
        put_symmetric(xs[s], fm[s])

    def sq(s):
        return square(xs[s], qs[s], ls[s])

    def norm(s):
        t00, t01, t11 = sq(s)
        total = t00 * t00 + 2.0 * (t01 * t01) + t11 * t11
        return jnp.sum(total, axis=(0, 1), keepdims=True)

    def tail(t, s):
        y = qs[s]
        v = fm[s, :B, :]
        w = 1.5 * v - 0.5 * rowmul(v, y)
        a = rowmul(w, y)
        a = 1.5 * a - 0.5 * rowmul(a, y)
        a = 1.5 * a - 0.5 * rowmul(a, y)
        z = 1.5 * w - 0.5 * a
        eye = (lax.broadcasted_iota(jnp.int32, (B, B), 0) == lax.broadcasted_iota(jnp.int32, (B, B), 1)).astype(f32)
        centre = 0.5 * (eye - z[:, blk[0]])
        dg[t, s] = 0.5 * (centre + centre.T)
        for k in range(1, 4):
            dct[t, s, k] = (-0.5 * present[s][k]) * z[:, blk[k]]

    for x in xs:
        x[...] = jnp.zeros_like(x)
    sm[...] = jnp.zeros_like(sm)
    load.wait()
    pl.semaphore_wait(barrier, ROWS + COLS - 2)

    for s in range(SLOTS):
        send(0, s)
    for s in range(SLOTS):
        relay(0, s)

    for t in range(STEPS):
        arrived(t, 0, (0, 1, 2, 4))
        assemble(t, 0)
        n0 = norm(0)
        if t == 1:
            relay(1, 1)
        cube(0)
        fourth(0)
        arrived(t, 1, (0, 1, 2, 4))
        assemble(t, 1)
        n1 = norm(1)
        own1[t] = jnp.broadcast_to(jnp.maximum(n0, n1), (8, 128))
        for k in row_order:
            maxcp(t, k).start()
        cube(1)
        fifth(0)
        fourth(1)
        seventh(0)
        for k in row_order:
            maxcp(t, k).wait_recv()
        top = own1[t]
        for k in row_order:
            top = jnp.maximum(top, mx1[t, k])
        own2[t] = top
        for k in col_order:
            maxcp(t, k).start()
        fifth(1)
        ninth(0)
        seventh(1)
        ninth(1)
        sent(t)
        for k in row_order:
            maxcp(t, k).wait_send()
        for k in col_order:
            maxcp(t, k).wait_recv()
            top = jnp.maximum(top, mx2[t, k - ROWS])
        scale = (1.5 / jnp.sqrt(jnp.sqrt(top + EPS)))[:1, :1]
        combine(0, scale)
        combine(1, scale)
        sq(0)

        def body(i, carry):
            advance(0)
            sq(1)
            sq(0)
            advance(1)
            return carry

        lax.fori_loop(0, 2, body, 0)
        tail(t, 0)
        send(t + 1, 0)
        sq(1)
        tail(t, 1)
        send(t + 1, 1)
        prepare(t, 0)
        relay(t + 1, 0)
        prepare(t, 1)
        for k in col_order:
            maxcp(t, k).wait_send()

    def finish(s):
        arrived(2, s, (0, 1, 2, 4))
        for k in range(1, 4):
            face = jnp.concatenate([got(2, s, k, 0), got(2, s, k, 1)], 0)
            out[s, k] = out[s, k] + (0.5 * present[s][k]) * face

    relay(2, 1)
    for s in range(SLOTS):
        finish(s)

    sent(STEPS)


def per_device(hamiltonian, block_lists):
    mat = pltpu.VMEM((N, N), f32)
    halves = pltpu.VMEM((N, 2 * N), bf16)
    return pl.pallas_call(
        kernel,
        out_shape=pltpu.VMEM((SLOTS, 4, B, B), f32),
        in_specs=[pl.BlockSpec(memory_space=pltpu.SMEM), pl.BlockSpec(memory_space=pl.ANY)],
        out_specs=pl.BlockSpec(memory_space=pltpu.VMEM),
        scratch_shapes=[
            pltpu.VMEM((SLOTS, 4, B, B), f32),
            pltpu.VMEM((5, SLOTS, 2, B, B), f32),
            pltpu.VMEM((5, SLOTS, 2, B, B), f32),
            pltpu.VMEM((5, SLOTS, 2, B // 2, B), f32),
            pltpu.VMEM((SLOTS, N, N), f32),
            pltpu.VMEM((SLOTS, N, N), f32),
            pltpu.VMEM((3, SLOTS, N, N), f32),
            halves, halves, mat, halves, halves, halves,
            halves, halves, mat, halves, halves, halves,
            pltpu.VMEM((STEPS, SLOTS, 4, B, B), f32),
            pltpu.VMEM((STEPS, SLOTS, B, B), f32),
            pltpu.VMEM((STEPS, 8, 128), f32),
            pltpu.VMEM((STEPS, 8, 128), f32),
            pltpu.VMEM((STEPS, ROWS, 8, 128), f32),
            pltpu.VMEM((STEPS, COLS, 8, 128), f32),
            pltpu.SemaphoreType.DMA,
            pltpu.SemaphoreType.DMA((3, 5, SLOTS, 4)),
            pltpu.SemaphoreType.DMA((3, 5, SLOTS, 4)),
            pltpu.SemaphoreType.DMA((STEPS, ROWS + COLS)),
            pltpu.SemaphoreType.DMA((STEPS, ROWS + COLS)),
        ],
        compiler_params=pltpu.CompilerParams(collective_id=0, has_side_effects=True),
    )(block_lists.T, hamiltonian)


def solution(mesh):
    return jax.shard_map(
        per_device,
        mesh=mesh,
        in_specs=(P(("row", "col"), None, None, None), P()),
        out_specs=P(("row", "col"), None, None, None),
        check_vma=False,
    )
```

```python
import jax
import jax.numpy as jnp
from jax import lax
from jax.experimental import pallas as pl
from jax.experimental.pallas import tpu as pltpu
from jax.sharding import PartitionSpec as P

STEPS = 2
SLOTS = 2
B = 128
N = 512
T = 256
EPS = 1e-06
ROWS = 8
COLS = 16
f32 = jnp.float32
bf16 = jnp.bfloat16
MESH = pl.DeviceIdType.MESH


def dot(a, b):
    return jnp.dot(a, b, preferred_element_type=f32)


def put(ref, r, c, x):
    m, n = x.shape
    h = x.astype(bf16)
    ref[r : r + m, c : c + n] = h
    ref[r : r + m, N + c : N + c + n] = (x - h.astype(f32)).astype(bf16)


def put_symmetric(ref, f):
    put(ref, 0, 0, f[:T, :T])
    upper = f[:T, T:]
    put(ref, 0, T, upper)
    put(ref, T, 0, upper.T)
    put(ref, T, T, f[T:, T:])


def square(x, q, low):
    low[...] = dot(x[:, :N], x[:, N:])
    a = dot(x[:T, :N], x[:, :T])
    t00 = a + low[:T, :T] + low[:T, :T].T
    put(q, 0, 0, t00)
    a = dot(x[:, :N], x[:, T:N])
    t01 = a[:T] + low[:T, T:] + low[T:, :T].T
    put(q, 0, T, t01)
    put(q, T, 0, t01.T)
    t11 = a[T:] + low[T:, T:] + low[T:, T:].T
    put(q, T, T, t11)
    return t00, t01, t11


def product(x, q, store):
    for m, c in ((T, 0), (N, T)):
        h, l = x[:m, :N], x[:m, N:]
        qh, ql = q[:, c : c + T], q[:, N + c : N + c + T]
        store(m, c, dot(jnp.concatenate([h, h, l], 1), jnp.concatenate([qh, ql, qh], 0)))


def rowmul(v, q):
    h = v.astype(bf16)
    l = (v - h.astype(f32)).astype(bf16)
    p = dot(jnp.concatenate([h, l], 0), q[:, :N])
    return p[:B] + p[B:] + dot(h, q[:, N:])


def kernel(
    lists, h_any, out, hv, rb0, rb1, rb2, sm, fm, pw, x0, q0, l0, c0, d0, e0, x1, q1, l1, c1, d1, e1, dct, dg, own1, own2, mx1, mx2,
    hsem, es, er, ms, mr,
):
    row, col = lax.axis_index("row"), lax.axis_index("col")
    rb = (rb0, rb1, rb2)
    xs, qs, ls = (x0, x1), (q0, q1), (l0, l1)
    thirds, fourths, fifths = (c0, c1), (d0, d1), (e0, e1)
    row_c = row + 1 - 2 * (row % 2)
    row_x = row + 2 - 4 * ((row // 2) % 2)
    row_f = (row_x + 4) % ROWS

    def row_peer(k):
        return (2 * ((row // 2 + k // 2) % 4) + (row % 2 + k % 2) % 2, col)

    def col_peer(k):
        return (row, 4 * ((col // 4 + k // 4) % 4) + (col % 4 + k % 4) % 4)

    def hops(n):
        return min(n, 4 - n)

    row_order = sorted(range(1, ROWS), key=lambda k: -hops(k // 2) - k % 2 / 4)
    col_order = [ROWS + k for k in sorted(range(1, COLS), key=lambda k: -hops(k // 4) - hops(k % 4))]

    load = pltpu.make_async_copy(h_any, hv, hsem)
    load.start()
    barrier = pltpu.get_barrier_semaphore()
    for k in col_order:
        pl.semaphore_signal(barrier, inc=1, device_id=col_peer(k - ROWS), device_id_type=MESH)
    for k in row_order:
        pl.semaphore_signal(barrier, inc=1, device_id=row_peer(k), device_id_type=MESH)

    def pieces(e, d):
        return 4 if d >= 3 and e < STEPS else 2

    def cp(e, d, s, c):
        target = (
            (row, (col + 1) % COLS),
            (row, (col + COLS - 1) % COLS),
            (row_c, col),
            (row_x, col),
            (row_f, col),
        )[d]
        face = (2, 1, 3, 3, 3)[d]
        half = B // 2
        fine = pieces(e, d) == 4
        q = c // 2 if fine else c
        part = pl.ds(half * (c % 2), half)
        if d == 4:
            src = rb[e].at[3, s, q]
        elif e == 0:
            src = hv.at[s, face if q else 0]
        elif e == 1:
            src = dct.at[0, s, face] if q else dg.at[0, s]
        else:
            src = dct.at[1, s, face, pl.ds(half * q, half)]
        dst = rb[e].at[d, s, q]
        return pltpu.make_async_remote_copy(
            src_ref=src.at[part] if fine else src,
            dst_ref=dst.at[part] if fine else dst,
            send_sem=es.at[e, d, s, c],
            recv_sem=er.at[e, d, s, c],
            device_id=target,
            device_id_type=MESH,
        )

    def send(e, s):
        for c in range(4):
            for d in (3, 0, 1, 2):
                if c < pieces(e, d):
                    cp(e, d, s, c).start()

    def relay(e, s):
        for c in range(pieces(e, 3)):
            cp(e, 3, s, c).wait_recv()
            cp(e, 4, s, c).start()

    def arrived(e, s, dirs):
        for d in dirs:
            for c in range(pieces(e, d)):
                cp(e, d, s, c).wait_recv()

    def sent(e):
        for s in range(SLOTS):
            for d in range(5):
                for c in range(pieces(e, d)):
                    cp(e, d, s, c).wait_send()

    def maxcp(t, k):
        if k < ROWS:
            src, dst, target = own1.at[t], mx1.at[t, k], row_peer(k)
        else:
            src, dst, target = own2.at[t], mx2.at[t, k - ROWS], col_peer(k - ROWS)
        return pltpu.make_async_remote_copy(
            src_ref=src, dst_ref=dst, send_sem=ms.at[t, k], recv_sem=mr.at[t, k], device_id=target, device_id_type=MESH
        )

    present, chosen = [], []
    for s in range(SLOTS):
        j = (row * COLS + col) * SLOTS + s
        present.append([1.0] + [jnp.where(lists[k, j] >= 0, 1.0, 0.0).astype(f32) for k in range(1, 4)])
        apart = jnp.abs(lists[3, j] // (SLOTS * COLS) - row)
        chosen.append((apart < 2, apart < 4))

    def got(e, s, k, q):
        if k < 3:
            return rb[e][k - 1, s, q]
        near, mid = chosen[s]
        return jnp.where(near, rb[e][2, s, q], jnp.where(mid, rb[e][3, s, q], rb[e][4, s, q]))

    blk = [slice(B * k, B * k + B) for k in range(4)]

    def assemble(t, s):
        x = xs[s]
        if t == 0:
            h = hv[s, 0]
            d = 0.5 * (h + h.T)
            sm[s, blk[0], blk[0]] = d
        else:
            d = sm[s, blk[0], blk[0]]
        put(x, 0, 0, d)
        for k in range(1, 4):
            p = present[s][k]
            diag, face = got(t, s, k, 0), got(t, s, k, 1)
            if t == 0:
                low = (0.5 * p) * (hv[s, k] + face.T)
                d = (0.5 * p) * (diag + diag.T)
            else:
                low = sm[s, blk[k], blk[0]] + (0.5 * p) * face
                d = sm[s, blk[k], blk[k]] + p * diag
            up = low.T
            sm[s, blk[k], blk[0]] = low
            sm[s, blk[0], blk[k]] = up
            sm[s, blk[k], blk[k]] = d
            put(x, B * k, 0, low)
            put(x, 0, B * k, up)
            put(x, B * k, B * k, d)

    def prepare(t, s):
        if t == 0:
            sm[s, blk[0], blk[0]] = sm[s, blk[0], blk[0]] + dg[0, s]
        else:
            out[s, 0] = dg[1, s]
        for k in range(1, 4):
            own = (0.5 * present[s][k]) * dct[t, s, k].T
            if t == 0:
                sm[s, blk[k], blk[0]] = sm[s, blk[k], blk[0]] + own
                for i in range(1, 4):
                    if i != k:
                        put(xs[s], B * k, B * i, jnp.zeros((B, B), f32))
            else:
                out[s, k] = own

    def combine(s, scale):
        two = scale * scale
        c1 = 2.25 * scale
        c3 = -2.4375 * scale * two
        c5 = 1.6875 * scale * (two * two)
        c7 = -0.5625 * scale * (two * two) * two
        c9 = 0.0625 * scale * (two * two) * (two * two)
        for r, c in ((0, 0), (0, T), (T, T)):
            at = (s, slice(r, r + T), slice(c, c + T))
            f = c1 * sm[at] + c3 * fm[at] + c5 * pw[(0, *at)] + c7 * pw[(1, *at)] + c9 * pw[(2, *at)]
            fm[at] = f
            put(xs[s], r, c, f)
            if r != c:
                put(xs[s], c, r, f.T)

    def power(a, b, s, dst, halves=None):
        def store(m, c, p):
            dst[s, :m, c : c + T] = p
            if halves is not None:
                put(halves, 0, c, p)
                if c:
                    put(halves, T, 0, p[:T].T)

        product(a, b, store)

    def cube(s):
        power(xs[s], qs[s], s, fm, thirds[s])

    def fourth(s):
        square(qs[s], fourths[s], ls[s])

    def fifth(s):
        power(thirds[s], qs[s], s, pw.at[0], fifths[s])

    def seventh(s):
        power(thirds[s], fourths[s], s, pw.at[1])

    def ninth(s):
        power(fifths[s], fourths[s], s, pw.at[2])

    def advance(s):
        def store(m, c, p):
            fm[s, :m, c : c + T] = 1.5 * fm[s, :m, c : c + T] - 0.5 * p

        product(xs[s], qs[s], store)
        put_symmetric(xs[s], fm[s])

    def sq(s):
        return square(xs[s], qs[s], ls[s])

    def norm(s):
        t00, t01, t11 = sq(s)
        total = t00 * t00 + 2.0 * (t01 * t01) + t11 * t11
        return jnp.sum(total, axis=(0, 1), keepdims=True)

    def tail(t, s):
        y = qs[s]
        v = fm[s, :B, :]
        w = 1.5 * v - 0.5 * rowmul(v, y)
        a = rowmul(w, y)
        a = 1.5 * a - 0.5 * rowmul(a, y)
        a = 1.5 * a - 0.5 * rowmul(a, y)
        z = 1.5 * w - 0.5 * a
        eye = (lax.broadcasted_iota(jnp.int32, (B, B), 0) == lax.broadcasted_iota(jnp.int32, (B, B), 1)).astype(f32)
        centre = 0.5 * (eye - z[:, blk[0]])
        dg[t, s] = 0.5 * (centre + centre.T)
        for k in range(1, 4):
            dct[t, s, k] = (-0.5 * present[s][k]) * z[:, blk[k]]

    for x in xs:
        x[...] = jnp.zeros_like(x)
    sm[...] = jnp.zeros_like(sm)
    load.wait()
    pl.semaphore_wait(barrier, ROWS + COLS - 2)

    for s in range(SLOTS):
        send(0, s)
    for s in range(SLOTS):
        relay(0, s)

    for t in range(STEPS):
        arrived(t, 0, (0, 1, 2, 4))
        assemble(t, 0)
        n0 = norm(0)
        cube(0)
        arrived(t, 1, (0, 1, 2, 4))
        assemble(t, 1)
        n1 = norm(1)
        own1[t] = jnp.broadcast_to(jnp.maximum(n0, n1), (8, 128))
        for k in row_order:
            maxcp(t, k).start()
        cube(1)
        fourth(0)
        fifth(0)
        fourth(1)
        seventh(0)
        for k in row_order:
            maxcp(t, k).wait_recv()
        top = own1[t]
        for k in row_order:
            top = jnp.maximum(top, mx1[t, k])
        own2[t] = top
        for k in col_order:
            maxcp(t, k).start()
        fifth(1)
        ninth(0)
        seventh(1)
        ninth(1)
        sent(t)
        for k in row_order:
            maxcp(t, k).wait_send()
        for k in col_order:
            maxcp(t, k).wait_recv()
            top = jnp.maximum(top, mx2[t, k - ROWS])
        scale = (1.5 / jnp.sqrt(jnp.sqrt(top + EPS)))[:1, :1]
        combine(0, scale)
        combine(1, scale)
        sq(0)

        def body(i, carry):
            advance(0)
            sq(1)
            sq(0)
            advance(1)
            return carry

        lax.fori_loop(0, 2, body, 0)
        tail(t, 0)
        send(t + 1, 0)
        sq(1)
        tail(t, 1)
        send(t + 1, 1)
        relay(t + 1, 0)
        prepare(t, 0)
        prepare(t, 1)
        relay(t + 1, 1)
        for k in col_order:
            maxcp(t, k).wait_send()

    def finish(s):
        arrived(2, s, (0, 1, 2, 4))
        for k in range(1, 4):
            face = jnp.concatenate([got(2, s, k, 0), got(2, s, k, 1)], 0)
            out[s, k] = out[s, k] + (0.5 * present[s][k]) * face

    for s in range(SLOTS):
        finish(s)

    sent(STEPS)


def per_device(hamiltonian, block_lists):
    mat = pltpu.VMEM((N, N), f32)
    halves = pltpu.VMEM((N, 2 * N), bf16)
    return pl.pallas_call(
        kernel,
        out_shape=pltpu.VMEM((SLOTS, 4, B, B), f32),
        in_specs=[pl.BlockSpec(memory_space=pltpu.SMEM), pl.BlockSpec(memory_space=pl.ANY)],
        out_specs=pl.BlockSpec(memory_space=pltpu.VMEM),
        scratch_shapes=[
            pltpu.VMEM((SLOTS, 4, B, B), f32),
            pltpu.VMEM((5, SLOTS, 2, B, B), f32),
            pltpu.VMEM((5, SLOTS, 2, B, B), f32),
            pltpu.VMEM((5, SLOTS, 2, B // 2, B), f32),
            pltpu.VMEM((SLOTS, N, N), f32),
            pltpu.VMEM((SLOTS, N, N), f32),
            pltpu.VMEM((3, SLOTS, N, N), f32),
            halves, halves, mat, halves, halves, halves,
            halves, halves, mat, halves, halves, halves,
            pltpu.VMEM((STEPS, SLOTS, 4, B, B), f32),
            pltpu.VMEM((STEPS, SLOTS, B, B), f32),
            pltpu.VMEM((STEPS, 8, 128), f32),
            pltpu.VMEM((STEPS, 8, 128), f32),
            pltpu.VMEM((STEPS, ROWS, 8, 128), f32),
            pltpu.VMEM((STEPS, COLS, 8, 128), f32),
            pltpu.SemaphoreType.DMA,
            pltpu.SemaphoreType.DMA((3, 5, SLOTS, 4)),
            pltpu.SemaphoreType.DMA((3, 5, SLOTS, 4)),
            pltpu.SemaphoreType.DMA((STEPS, ROWS + COLS)),
            pltpu.SemaphoreType.DMA((STEPS, ROWS + COLS)),
        ],
        compiler_params=pltpu.CompilerParams(collective_id=0, has_side_effects=True),
    )(block_lists.T, hamiltonian)


def solution(mesh):
    return jax.shard_map(
        per_device,
        mesh=mesh,
        in_specs=(P(("row", "col"), None, None, None), P()),
        out_specs=P(("row", "col"), None, None, None),
        check_vma=False,
    )
```

```python
import jax
import jax.numpy as jnp
from jax import lax
from jax.experimental import pallas as pl
from jax.experimental.pallas import tpu as pltpu
from jax.sharding import PartitionSpec as P

STEPS = 2
SLOTS = 2
B = 128
N = 512
T = 256
EPS = 1e-06
ROWS = 8
COLS = 16
f32 = jnp.float32
bf16 = jnp.bfloat16
MESH = pl.DeviceIdType.MESH


def dot(a, b):
    return jnp.dot(a, b, preferred_element_type=f32)


def put(ref, r, c, x):
    m, n = x.shape
    h = x.astype(bf16)
    ref[r : r + m, c : c + n] = h
    ref[r : r + m, N + c : N + c + n] = (x - h.astype(f32)).astype(bf16)


def put_symmetric(ref, f):
    put(ref, 0, 0, f[:T, :T])
    upper = f[:T, T:]
    put(ref, 0, T, upper)
    put(ref, T, 0, upper.T)
    put(ref, T, T, f[T:, T:])


def square(x, q, low):
    low[...] = dot(x[:, :N], x[:, N:])
    a = dot(x[:T, :N], x[:, :T])
    t00 = a + low[:T, :T] + low[:T, :T].T
    put(q, 0, 0, t00)
    a = dot(x[:, :N], x[:, T:N])
    t01 = a[:T] + low[:T, T:] + low[T:, :T].T
    put(q, 0, T, t01)
    put(q, T, 0, t01.T)
    t11 = a[T:] + low[T:, T:] + low[T:, T:].T
    put(q, T, T, t11)
    return t00, t01, t11


def product(x, q, store):
    for m, c in ((T, 0), (N, T)):
        h, l = x[:m, :N], x[:m, N:]
        qh, ql = q[:, c : c + T], q[:, N + c : N + c + T]
        store(m, c, dot(jnp.concatenate([h, h, l], 1), jnp.concatenate([qh, ql, qh], 0)))


def rowmul(v, q):
    h = v.astype(bf16)
    l = (v - h.astype(f32)).astype(bf16)
    p = dot(jnp.concatenate([h, l], 0), q[:, :N])
    return p[:B] + p[B:] + dot(h, q[:, N:])


def kernel(
    lists, h_any, out, hv, rb0, rb1, rb2, sm, fm, pw, x0, q0, l0, c0, d0, e0, x1, q1, l1, c1, d1, e1, dct, dg, own1, own2, mx1, mx2,
    hsem, es, er, ms, mr,
):
    row, col = lax.axis_index("row"), lax.axis_index("col")
    rb = (rb0, rb1, rb2)
    xs, qs, ls = (x0, x1), (q0, q1), (l0, l1)
    thirds, fourths, fifths = (c0, c1), (d0, d1), (e0, e1)
    row_c = row + 1 - 2 * (row % 2)
    row_x = row + 2 - 4 * ((row // 2) % 2)
    row_f = (row_x + 4) % ROWS

    def row_peer(k):
        return (2 * ((row // 2 + k // 2) % 4) + (row % 2 + k % 2) % 2, col)

    def col_peer(k):
        return (row, 4 * ((col // 4 + k // 4) % 4) + (col % 4 + k % 4) % 4)

    def hops(n):
        return min(n, 4 - n)

    row_order = sorted(range(1, ROWS), key=lambda k: -hops(k // 2) - k % 2 / 4)
    col_order = [ROWS + k for k in sorted(range(1, COLS), key=lambda k: -hops(k // 4) - hops(k % 4))]

    load = pltpu.make_async_copy(h_any, hv, hsem)
    load.start()
    barrier = pltpu.get_barrier_semaphore()
    for k in col_order:
        pl.semaphore_signal(barrier, inc=1, device_id=col_peer(k - ROWS), device_id_type=MESH)
    for k in row_order:
        pl.semaphore_signal(barrier, inc=1, device_id=row_peer(k), device_id_type=MESH)

    def pieces(e, d):
        return 4 if d >= 3 else 2

    def cp(e, d, s, c):
        target = (
            (row, (col + 1) % COLS),
            (row, (col + COLS - 1) % COLS),
            (row_c, col),
            (row_x, col),
            (row_f, col),
        )[d]
        face = (2, 1, 3, 3, 3)[d]
        half = B // 2
        fine = pieces(e, d) == 4
        q = c // 2 if fine else c
        size = half if e < STEPS else half // 2
        part = pl.ds(size * (c % 2), size)
        if d == 4:
            src = rb[e].at[3, s, q]
        elif e == 0:
            src = hv.at[s, face if q else 0]
        elif e == 1:
            src = dct.at[0, s, face] if q else dg.at[0, s]
        else:
            src = dct.at[1, s, face, pl.ds(half * q, half)]
        dst = rb[e].at[d, s, q]
        return pltpu.make_async_remote_copy(
            src_ref=src.at[part] if fine else src,
            dst_ref=dst.at[part] if fine else dst,
            send_sem=es.at[e, d, s, c],
            recv_sem=er.at[e, d, s, c],
            device_id=target,
            device_id_type=MESH,
        )

    def send(e, s):
        for c in range(4):
            for d in (3, 0, 1, 2):
                if c < pieces(e, d):
                    cp(e, d, s, c).start()

    def relay(e, s):
        for c in range(pieces(e, 3)):
            cp(e, 3, s, c).wait_recv()
            cp(e, 4, s, c).start()

    def arrived(e, s, dirs):
        for d in dirs:
            for c in range(pieces(e, d)):
                cp(e, d, s, c).wait_recv()

    def sent(e):
        for s in range(SLOTS):
            for d in range(5):
                for c in range(pieces(e, d)):
                    cp(e, d, s, c).wait_send()

    def maxcp(t, k):
        if k < ROWS:
            src, dst, target = own1.at[t], mx1.at[t, k], row_peer(k)
        else:
            src, dst, target = own2.at[t], mx2.at[t, k - ROWS], col_peer(k - ROWS)
        return pltpu.make_async_remote_copy(
            src_ref=src, dst_ref=dst, send_sem=ms.at[t, k], recv_sem=mr.at[t, k], device_id=target, device_id_type=MESH
        )

    present, chosen = [], []
    for s in range(SLOTS):
        j = (row * COLS + col) * SLOTS + s
        present.append([1.0] + [jnp.where(lists[k, j] >= 0, 1.0, 0.0).astype(f32) for k in range(1, 4)])
        apart = jnp.abs(lists[3, j] // (SLOTS * COLS) - row)
        chosen.append((apart < 2, apart < 4))

    def got(e, s, k, q):
        if k < 3:
            return rb[e][k - 1, s, q]
        near, mid = chosen[s]
        return jnp.where(near, rb[e][2, s, q], jnp.where(mid, rb[e][3, s, q], rb[e][4, s, q]))

    blk = [slice(B * k, B * k + B) for k in range(4)]

    def assemble(t, s):
        x = xs[s]
        if t == 0:
            h = hv[s, 0]
            d = 0.5 * (h + h.T)
            sm[s, blk[0], blk[0]] = d
        else:
            d = sm[s, blk[0], blk[0]]
        put(x, 0, 0, d)
        for k in range(1, 4):
            p = present[s][k]
            diag, face = got(t, s, k, 0), got(t, s, k, 1)
            if t == 0:
                low = (0.5 * p) * (hv[s, k] + face.T)
                d = (0.5 * p) * (diag + diag.T)
            else:
                low = sm[s, blk[k], blk[0]] + (0.5 * p) * face
                d = sm[s, blk[k], blk[k]] + p * diag
            up = low.T
            sm[s, blk[k], blk[0]] = low
            sm[s, blk[0], blk[k]] = up
            sm[s, blk[k], blk[k]] = d
            put(x, B * k, 0, low)
            put(x, 0, B * k, up)
            put(x, B * k, B * k, d)

    def prepare(t, s):
        if t == 0:
            sm[s, blk[0], blk[0]] = sm[s, blk[0], blk[0]] + dg[0, s]
        else:
            out[s, 0] = dg[1, s]
        for k in range(1, 4):
            own = (0.5 * present[s][k]) * dct[t, s, k].T
            if t == 0:
                sm[s, blk[k], blk[0]] = sm[s, blk[k], blk[0]] + own
                for i in range(1, 4):
                    if i != k:
                        put(xs[s], B * k, B * i, jnp.zeros((B, B), f32))
            else:
                out[s, k] = own

    def combine(s, scale):
        two = scale * scale
        c1 = 2.25 * scale
        c3 = -2.4375 * scale * two
        c5 = 1.6875 * scale * (two * two)
        c7 = -0.5625 * scale * (two * two) * two
        c9 = 0.0625 * scale * (two * two) * (two * two)
        for r, c in ((0, 0), (0, T), (T, T)):
            at = (s, slice(r, r + T), slice(c, c + T))
            f = c1 * sm[at] + c3 * fm[at] + c5 * pw[(0, *at)] + c7 * pw[(1, *at)] + c9 * pw[(2, *at)]
            fm[at] = f
            put(xs[s], r, c, f)
            if r != c:
                put(xs[s], c, r, f.T)

    def power(a, b, s, dst, halves=None):
        def store(m, c, p):
            dst[s, :m, c : c + T] = p
            if halves is not None:
                put(halves, 0, c, p)
                if c:
                    put(halves, T, 0, p[:T].T)

        product(a, b, store)

    def cube(s):
        power(xs[s], qs[s], s, fm, thirds[s])

    def fourth(s):
        square(qs[s], fourths[s], ls[s])

    def fifth(s):
        power(thirds[s], qs[s], s, pw.at[0], fifths[s])

    def seventh(s):
        power(thirds[s], fourths[s], s, pw.at[1])

    def ninth(s):
        power(fifths[s], fourths[s], s, pw.at[2])

    def advance(s):
        def store(m, c, p):
            fm[s, :m, c : c + T] = 1.5 * fm[s, :m, c : c + T] - 0.5 * p

        product(xs[s], qs[s], store)
        put_symmetric(xs[s], fm[s])

    def sq(s):
        return square(xs[s], qs[s], ls[s])

    def norm(s):
        t00, t01, t11 = sq(s)
        total = t00 * t00 + 2.0 * (t01 * t01) + t11 * t11
        return jnp.sum(total, axis=(0, 1), keepdims=True)

    def tail(t, s):
        y = qs[s]
        v = fm[s, :B, :]
        w = 1.5 * v - 0.5 * rowmul(v, y)
        a = rowmul(w, y)
        a = 1.5 * a - 0.5 * rowmul(a, y)
        a = 1.5 * a - 0.5 * rowmul(a, y)
        z = 1.5 * w - 0.5 * a
        eye = (lax.broadcasted_iota(jnp.int32, (B, B), 0) == lax.broadcasted_iota(jnp.int32, (B, B), 1)).astype(f32)
        centre = 0.5 * (eye - z[:, blk[0]])
        dg[t, s] = 0.5 * (centre + centre.T)
        for k in range(1, 4):
            dct[t, s, k] = (-0.5 * present[s][k]) * z[:, blk[k]]

    for x in xs:
        x[...] = jnp.zeros_like(x)
    sm[...] = jnp.zeros_like(sm)
    load.wait()
    pl.semaphore_wait(barrier, ROWS + COLS - 2)

    for s in range(SLOTS):
        send(0, s)
    for s in range(SLOTS):
        relay(0, s)

    for t in range(STEPS):
        arrived(t, 0, (0, 1, 2, 4))
        assemble(t, 0)
        n0 = norm(0)
        cube(0)
        arrived(t, 1, (0, 1, 2, 4))
        assemble(t, 1)
        n1 = norm(1)
        own1[t] = jnp.broadcast_to(jnp.maximum(n0, n1), (1, 128))
        for k in row_order:
            maxcp(t, k).start()
        cube(1)
        fourth(0)
        fifth(0)
        fourth(1)
        seventh(0)
        for k in row_order:
            maxcp(t, k).wait_recv()
        top = own1[t]
        for k in row_order:
            top = jnp.maximum(top, mx1[t, k])
        own2[t] = top
        for k in col_order:
            maxcp(t, k).start()
        fifth(1)
        ninth(0)
        seventh(1)
        ninth(1)
        sent(t)
        for k in row_order:
            maxcp(t, k).wait_send()
        for k in col_order:
            maxcp(t, k).wait_recv()
            top = jnp.maximum(top, mx2[t, k - ROWS])
        scale = (1.5 / jnp.sqrt(jnp.sqrt(top + EPS)))[:1, :1]
        combine(0, scale)
        combine(1, scale)
        sq(0)

        def body(i, carry):
            advance(0)
            sq(1)
            sq(0)
            advance(1)
            return carry

        lax.fori_loop(0, 2, body, 0)
        tail(t, 0)
        send(t + 1, 0)
        sq(1)
        tail(t, 1)
        send(t + 1, 1)
        relay(t + 1, 0)
        prepare(t, 0)
        prepare(t, 1)
        relay(t + 1, 1)
        for k in col_order:
            maxcp(t, k).wait_send()

    def finish(s):
        arrived(2, s, (0, 1, 2, 4))
        for k in range(1, 4):
            face = jnp.concatenate([got(2, s, k, 0), got(2, s, k, 1)], 0)
            out[s, k] = out[s, k] + (0.5 * present[s][k]) * face

    for s in range(SLOTS):
        finish(s)

    sent(STEPS)


def per_device(hamiltonian, block_lists):
    mat = pltpu.VMEM((N, N), f32)
    halves = pltpu.VMEM((N, 2 * N), bf16)
    return pl.pallas_call(
        kernel,
        out_shape=pltpu.VMEM((SLOTS, 4, B, B), f32),
        in_specs=[pl.BlockSpec(memory_space=pltpu.SMEM), pl.BlockSpec(memory_space=pl.ANY)],
        out_specs=pl.BlockSpec(memory_space=pltpu.VMEM),
        scratch_shapes=[
            pltpu.VMEM((SLOTS, 4, B, B), f32),
            pltpu.VMEM((5, SLOTS, 2, B, B), f32),
            pltpu.VMEM((5, SLOTS, 2, B, B), f32),
            pltpu.VMEM((5, SLOTS, 2, B // 2, B), f32),
            pltpu.VMEM((SLOTS, N, N), f32),
            pltpu.VMEM((SLOTS, N, N), f32),
            pltpu.VMEM((3, SLOTS, N, N), f32),
            halves, halves, mat, halves, halves, halves,
            halves, halves, mat, halves, halves, halves,
            pltpu.VMEM((STEPS, SLOTS, 4, B, B), f32),
            pltpu.VMEM((STEPS, SLOTS, B, B), f32),
            pltpu.VMEM((STEPS, 1, 128), f32),
            pltpu.VMEM((STEPS, 1, 128), f32),
            pltpu.VMEM((STEPS, ROWS, 1, 128), f32),
            pltpu.VMEM((STEPS, COLS, 1, 128), f32),
            pltpu.SemaphoreType.DMA,
            pltpu.SemaphoreType.DMA((3, 5, SLOTS, 4)),
            pltpu.SemaphoreType.DMA((3, 5, SLOTS, 4)),
            pltpu.SemaphoreType.DMA((STEPS, ROWS + COLS)),
            pltpu.SemaphoreType.DMA((STEPS, ROWS + COLS)),
        ],
        compiler_params=pltpu.CompilerParams(collective_id=0, has_side_effects=True),
    )(block_lists.T, hamiltonian)


def solution(mesh):
    return jax.shard_map(
        per_device,
        mesh=mesh,
        in_specs=(P(("row", "col"), None, None, None), P()),
        out_specs=P(("row", "col"), None, None, None),
        check_vma=False,
    )
```
